128 devices in a mesh: expert: 32 (over z, x, core), width: 4 (over y).
Axes of the slice: x: 4, y: 4, z: 4, core: 2. Of those that a mesh axis runs over, the one named last changes fastest.
Arguments:
- tokens: bfloat16 [4096, 4096], P('expert'), may hold values from -6 to 6
- expert_ids: int32 [4096, 8], P('expert'), may hold values from 0 to 63, all different within a row; in each aligned block of 128 rows (0 to 127, 128 to 255, ...) at most 32 rows name the same one
- combine_weights: float32 [4096, 8], P('expert'), may hold values from 0.05 to 0.3
- gate_weight: bfloat16 [64, 4096, 1536], P('expert', None, 'width'), may hold values from -0.09375 to 0.09375
- up_weight: bfloat16 [64, 4096, 1536], P('expert', None, 'width'), may hold values from -0.09375 to 0.09375
- down_weight: bfloat16 [64, 1536, 4096], P('expert', 'width'), may hold values from -0.15625 to 0.15625
Outputs:
- mixed: bfloat16 [4096, 4096], P('expert', 'width')
The draws below stay inside these ranges and needn't reach their ends.
Inputs may be any that keep to these rules, and one draw needn't show every extreme that they name: `expert_ids`: each token names 8 different experts. Within the tokens of one index of expert (aligned blocks of 128 tokens) no expert is named by more than 32 tokens, a bound that some block reaches.
All inputs are finite; a program needn't handle non-finite values.
Results may differ from the reference program's by a relative error of at most 0.012.
Values may be sent and summed in bfloat16 or wider, within the bound.
No kernel may reach another device: no remote copies, remote signals or barrier semaphores. Data moves between devices by JAX's collectives and lax.ppermute only.
A program may use at most 128 MiB of HBM per device.

```python
import math
import jax
import jax.numpy as jnp
import numpy as np
from jax import lax

D = 4096
FF = 1536
TOP = 8
TOK_DEV = 128
EXPERTS = 64
TOKENS = 4096
MOST = 32
N_EXPERT = 32
N_WIDTH = 4


def block_scale(key, extent, cuts, least, largest):
    loudness = 1.0
    for position, shards_of in cuts:
        steps = jax.random.uniform(jax.random.fold_in(jax.random.fold_in(key, 6), position), (shards_of,), jnp.float32, least / len(cuts), largest / len(cuts))
        loudness = loudness * jnp.repeat(jnp.exp(steps), extent[position] // shards_of).reshape((-1,) + (1,) * (len(extent) - 1 - position))
    return loudness


def deal_out(stream_key, own, number, rows, count, top, reach, slope):
    ranking = jax.random.permutation(stream_key, count)
    crowded, common = shares(count, rows * top, reach, slope, True), shares(count, rows * top, reach, slope, False)
    places = jnp.arange(count)

    def named(sizes, offset_by):
        used = int((sizes > 0).sum())
        fixed = max(1, used // 4)
        moved = fixed + (places - fixed + offset_by * (used - fixed)) % max(1, count - fixed)
        return jnp.zeros((count,), jnp.int32).at[ranking[jnp.where(places < fixed, places, moved)]].set(jnp.asarray(sizes, jnp.int32))

    sizes = jnp.where(number % 4 == 0, named(crowded, number // 4), named(common, number - number // 4 - 1))
    mixed = jax.random.permutation(jax.random.fold_in(own, 3), count)
    source_of, sink = mixed[0:count // 2 * 2:2], mixed[1:count // 2 * 2:2]
    room = jnp.minimum(sizes[source_of] - 1, reach - sizes[sink]) // 2
    room = jnp.where((source_of == ranking[0]) | (sink == ranking[0]) | (sizes[sink] == 0), 0, jnp.maximum(room, 0))
    moved = jax.random.randint(jax.random.fold_in(own, 4), (count // 2,), 0, 1 << 20) % (room + 1)
    sizes = sizes.at[source_of].add(-moved).at[sink].add(moved)
    members = jnp.searchsorted(jnp.cumsum(sizes), jnp.arange(rows * top), side="right").astype(jnp.int32)
    listing = members.reshape(top, rows).T
    listing = listing[jax.random.permutation(jax.random.fold_in(own, 1), rows)]
    offset_by = jax.random.randint(jax.random.fold_in(own, 2), (rows, 1), 0, top)
    return jnp.take_along_axis(listing, (jnp.arange(top)[None, :] + offset_by) % top, axis=1)


def shares(number_of, total, bound, skew, full):
    portions = [(1 << 20) // math.isqrt(grade ** skew) + 1 for grade in range(1, number_of + 1)]
    largest = bound if full else min(bound, max(-(-total // number_of), total * portions[0] // sum(portions)))
    least = 1 if total - largest >= number_of - 1 else 0
    given, spare = [largest] + [least] * (number_of - 1), total - largest - least * (number_of - 1)
    while spare > 0:
        movable = [i for i in range(1, number_of) if given[i] < largest] or [i for i in range(1, number_of) if given[i] < bound]
        pool, remaining = sum([portions[i] for i in movable]), spare
        for i in movable:
            addition = min(bound - given[i], max(1, remaining * portions[i] // pool), spare)
            given[i] = given[i] + addition
            spare = spare - addition
    return np.array(given)


def scatter_about(own_key, shape, deviation, limit, pieces=(), kind=jnp.bfloat16):
    result = jax.random.normal(own_key, shape, jnp.float32) * deviation
    if len(pieces) > 0:
        result = block_scale(own_key, shape, pieces, -0.22, 0.18) * result
    return jnp.clip(result, min=-limit, max=limit).astype(kind)


def setup_inputs(seed: int = 0) -> dict:
    key_list = jax.random.split(jax.random.key(seed), 7)
    tokens = scatter_about(key_list[0], (TOKENS, D), 1.0, 6.0, ((0, 32),))
    expert_ids_keys = jax.random.split(jax.random.fold_in(key_list[1], 1), TOKENS // TOK_DEV)
    expert_ids_turns = jax.random.permutation(jax.random.fold_in(key_list[1], 3), TOKENS // TOK_DEV)
    expert_ids = jax.vmap(lambda own, number: deal_out(jax.random.fold_in(key_list[1], 2), own, number, TOK_DEV, EXPERTS, TOP, MOST, 1))(expert_ids_keys, expert_ids_turns).reshape((TOKENS, TOP))
    combine_weights = jnp.clip(0.05 + 0.25 * jax.random.uniform(key_list[2], (TOKENS, TOP), jnp.float32) ** block_scale(key_list[2], (TOKENS, TOP), ((0, 32),), -0.2, 0.2), 0.05, 0.3)
    gate_weight = scatter_about(key_list[3], (EXPERTS, D, FF), D ** -0.5, 0.09375, ((0, 32), (2, 4)))
    up_weight = scatter_about(key_list[4], (EXPERTS, D, FF), D ** -0.5, 0.09375, ((0, 32), (2, 4)))
    down_weight = scatter_about(key_list[5], (EXPERTS, FF, D), FF ** -0.5, 0.15625, ((0, 32), (1, 4)))
    return dict(tokens=tokens, expert_ids=expert_ids, combine_weights=combine_weights, gate_weight=gate_weight, up_weight=up_weight, down_weight=down_weight)


def ranks_of(expert_ids):
    flat_ids = expert_ids.reshape(N_EXPERT, TOK_DEV * TOP)
    onehot = (flat_ids[:, :, None] == jnp.arange(EXPERTS, dtype=jnp.int32)[None, None, :]).astype(jnp.int32)
    counted = jnp.cumsum(onehot, axis=1)
    return jnp.sum(counted * onehot, axis=2).astype(jnp.int32) - 1


def reference(tokens, expert_ids, combine_weights, gate_weight, up_weight, down_weight):
    rank = ranks_of(expert_ids)
    flat_ids = expert_ids.reshape(N_EXPERT, TOK_DEV * TOP)
    source = jnp.arange(N_EXPERT, dtype=jnp.int32)[:, None]
    slot = flat_ids * (N_EXPERT * MOST) + source * MOST + rank
    token_index = source * TOK_DEV + jnp.arange(TOK_DEV * TOP, dtype=jnp.int32)[None, :] // TOP
    table = jnp.full((EXPERTS * N_EXPERT * MOST,), TOKENS, jnp.int32)
    table = table.at[slot.reshape(-1)].set(token_index.reshape(-1))
    padded = jnp.concatenate([tokens, jnp.zeros((1, D), jnp.bfloat16)], axis=0)
    group = FF // N_WIDTH

    def one_expert(packed):
        gate_one, up_one, down_one, rows_index = packed
        rows = padded[rows_index]
        total = jnp.zeros((rows.shape[0], D), jnp.float32)
        for index in range(N_WIDTH):
            gate = jnp.dot(rows, gate_one[:, index * group:(index + 1) * group], preferred_element_type=jnp.float32)
            up = jnp.dot(rows, up_one[:, index * group:(index + 1) * group], preferred_element_type=jnp.float32)
            hidden = (jax.nn.silu(gate) * up).astype(jnp.bfloat16)
            partial_value = jnp.dot(hidden, down_one[index * group:(index + 1) * group, :], preferred_element_type=jnp.float32)
            total = total + partial_value.astype(jnp.bfloat16).astype(jnp.float32)
        return total

    outputs = lax.map(one_expert, (gate_weight, up_weight, down_weight, table.reshape(EXPERTS, N_EXPERT * MOST)))
    outputs = outputs.reshape(EXPERTS * N_EXPERT * MOST, D)
    slot_tokens = slot.reshape(TOKENS, TOP)
    mixed = jnp.zeros((TOKENS, D), jnp.float32)
    for choice_index in range(TOP):
        mixed = mixed + combine_weights[:, choice_index:choice_index + 1] * outputs[slot_tokens[:, choice_index]]
    return mixed.astype(jnp.bfloat16)
```

```python
import jax
import jax.numpy as jnp
from jax import lax
from jax.experimental import pallas as pl
from jax.experimental.pallas import tpu as pltpu
from jax.sharding import PartitionSpec as P

MOST = 32
VMEM_BYTES = 60 * 1024 * 1024


def gate_up_body(group, slots, x_ref, q_ref, gate_ref, up_ref, out_ref, rows_ref):
    tok = x_ref.shape[0] // group
    exp_local, width_all, _ = gate_ref.shape
    place = lax.broadcasted_iota(jnp.int32, (slots, tok), 0)
    for b in range(group):
        pick = jnp.concatenate(
            [
                jnp.where(place == q_ref[b, j][None, :], 1.0, 0.0).astype(jnp.bfloat16)
                for j in range(exp_local)
            ],
            axis=0,
        )
        for c in range(0, width_all, 1024):
            rows = jnp.dot(
                pick,
                x_ref[b * tok : (b + 1) * tok, c : c + 1024],
                preferred_element_type=jnp.float32,
            ).astype(jnp.bfloat16)
            for j in range(exp_local):
                rows_ref[j, b * slots : (b + 1) * slots, c : c + 1024] = rows[
                    j * slots : (j + 1) * slots
                ]
    for j in range(exp_local):
        rows = rows_ref[j]
        gate = jnp.dot(rows, gate_ref[j], preferred_element_type=jnp.float32)
        up = jnp.dot(rows, up_ref[j], preferred_element_type=jnp.float32)
        hidden = (jax.nn.silu(gate) * up).astype(jnp.bfloat16)
        out_ref[:, j] = hidden.reshape(group, slots, hidden.shape[-1])


def gate_up(x_all, q_in, gate_weight, up_weight, slots, group=8):
    sources, exp_local, tok = q_in.shape
    _, width_all, hid = gate_weight.shape
    weight_spec = pl.BlockSpec(
        (exp_local, width_all, hid), lambda i: (0, 0, 0), pipeline_mode=pl.Buffered(1)
    )
    return pl.pallas_call(
        lambda *refs: gate_up_body(group, slots, *refs),
        out_shape=jax.ShapeDtypeStruct((sources, exp_local, slots, hid), jnp.bfloat16),
        grid=(sources // group,),
        in_specs=[
            pl.BlockSpec((group * tok, width_all), lambda i: (i, 0)),
            pl.BlockSpec((group, exp_local, tok), lambda i: (i, 0, 0)),
            weight_spec,
            weight_spec,
        ],
        out_specs=pl.BlockSpec((group, exp_local, slots, hid), lambda i: (i, 0, 0, 0)),
        scratch_shapes=[pltpu.VMEM((exp_local, group * slots, width_all), jnp.bfloat16)],
        compiler_params=pltpu.CompilerParams(vmem_limit_bytes=VMEM_BYTES),
        name="gate_up",
    )(x_all, q_in, gate_weight, up_weight)


def down_body(h_ref, w_ref, out_ref):
    n_width, group, exp_local, slots, hid = h_ref.shape
    cols = w_ref.shape[-1]
    for j in range(exp_local):
        total = jnp.zeros((group * slots, cols), jnp.float32)
        for y in range(n_width):
            total = total + jnp.dot(
                h_ref[y, :, j].reshape(group * slots, hid),
                w_ref[y, j],
                preferred_element_type=jnp.float32,
            )
        out_ref[:, j] = total.astype(jnp.bfloat16).reshape(group, slots, cols)


def down(h_all, weight, group=8):
    n_width, sources, exp_local, slots, hid = h_all.shape
    cols = weight.shape[-1]
    return pl.pallas_call(
        down_body,
        out_shape=jax.ShapeDtypeStruct((sources, exp_local, slots, cols), jnp.bfloat16),
        grid=(sources // group,),
        in_specs=[
            pl.BlockSpec((n_width, group, exp_local, slots, hid), lambda i: (0, i, 0, 0, 0)),
            pl.BlockSpec(
                (n_width, exp_local, hid, cols),
                lambda i: (0, 0, 0, 0),
                pipeline_mode=pl.Buffered(1),
            ),
        ],
        out_specs=pl.BlockSpec((group, exp_local, slots, cols), lambda i: (i, 0, 0, 0)),
        compiler_params=pltpu.CompilerParams(vmem_limit_bytes=VMEM_BYTES),
        name="down",
    )(h_all, weight)


def local(tokens, expert_ids, combine_weights, gate_weight, up_weight, down_weight):
    tok_rows = tokens.shape[0]
    exp_local = gate_weight.shape[0]
    n_expert = lax.axis_size("expert")
    experts_all = exp_local * n_expert
    slots = min(MOST, tok_rows)

    x_all = lax.all_gather(tokens, "expert", axis=0, tiled=True)

    experts = jnp.arange(experts_all, dtype=jnp.int32)
    hit = expert_ids.T[:, None, :] == experts[None, :, None]
    member = jnp.any(hit, axis=0)
    weight_of = jnp.sum(jnp.where(hit, combine_weights.T[:, None, :], 0.0), axis=0)
    order = jnp.arange(tok_rows, dtype=jnp.int32)
    earlier = (order[:, None] < order[None, :]).astype(jnp.bfloat16)
    rank = jnp.dot(member.astype(jnp.bfloat16), earlier, preferred_element_type=jnp.float32)
    place = jnp.where(member, rank.astype(jnp.int32), -1)
    q_in = lax.all_to_all(
        place.reshape(n_expert, exp_local, tok_rows), "expert", split_axis=0, concat_axis=0, tiled=True
    )
    seat = place[:, None, :] == jnp.arange(slots, dtype=jnp.int32)[None, :, None]
    spread = jnp.where(seat, weight_of[:, None, :], 0.0).reshape(experts_all * slots, tok_rows)
    high = spread.astype(jnp.bfloat16)
    low = (spread - high.astype(jnp.float32)).astype(jnp.bfloat16)

    n_width = lax.axis_size("width")
    hid, width_all = down_weight.shape[1:]
    cut = down_weight.reshape(exp_local, hid, n_width, width_all // n_width).transpose(2, 0, 1, 3)
    down_cols = lax.all_to_all(cut, "width", split_axis=0, concat_axis=0, tiled=True)
    x_all, q_in, down_cols = lax.optimization_barrier((x_all, q_in, down_cols))

    hidden = gate_up(x_all, q_in, gate_weight, up_weight, slots)
    h_all = lax.all_gather(hidden, "width", axis=0, tiled=False)
    rows = down(h_all, down_cols)
    returned = lax.all_to_all(rows, "expert", split_axis=0, concat_axis=0, tiled=True)
    returned = returned.reshape(experts_all * slots, rows.shape[-1])
    both = jnp.concatenate([high, low], axis=1)
    mixed = lax.dot_general(
        both, returned, (((0,), (0,)), ((), ())), preferred_element_type=jnp.float32
    )
    return (mixed[:tok_rows] + mixed[tok_rows:]).astype(jnp.bfloat16)


def solution(mesh):
    placed = (
        P("expert", None),
        P("expert", None),
        P("expert", None),
        P("expert", None, "width"),
        P("expert", None, "width"),
        P("expert", "width", None),
    )
    return jax.shard_map(
        local, mesh=mesh, in_specs=placed, out_specs=P("expert", "width"), check_vma=False
    )
```

```python
import jax
import jax.numpy as jnp
from jax import lax
from jax.experimental import pallas as pl
from jax.experimental.pallas import tpu as pltpu
from jax.sharding import PartitionSpec as P

MOST = 32
SIDE = 4
STEPS = 4
VMEM_BYTES = 56 * 1024 * 1024


def gate_up_body(slots, ids_ref, q_ref, *refs):
    parts = refs[:4]
    gate_ref, up_ref, out_ref, rows_ref, gate_acc, up_acc = refs[4:]
    step = pl.program_id(0)
    tok = q_ref.shape[-1]
    exp_local = gate_ref.shape[0]
    each = parts[0].shape[0] // tok
    place = lax.broadcasted_iota(jnp.int32, (slots, tok), 0)

    @pl.when(step == 0)
    def _():
        gate_acc[...] = jnp.zeros_like(gate_acc)
        up_acc[...] = jnp.zeros_like(up_acc)

    for b in range(4 * each):
        seats = q_ref[ids_ref[b]]
        pick = jnp.concatenate(
            [
                jnp.where(place == seats[j][None, :], 1.0, 0.0).astype(jnp.bfloat16)
                for j in range(exp_local)
            ],
            axis=0,
        )
        at = (b % each) * tok
        rows = jnp.dot(
            pick, parts[b // each][at : at + tok, :], preferred_element_type=jnp.float32
        ).astype(jnp.bfloat16)
        for j in range(exp_local):
            rows_ref[j, b * slots : (b + 1) * slots, :] = rows[j * slots : (j + 1) * slots]
    for j in range(exp_local):
        rows = rows_ref[j]
        gate_acc[j] += jnp.dot(rows, gate_ref[j], preferred_element_type=jnp.float32)
        up_acc[j] += jnp.dot(rows, up_ref[j], preferred_element_type=jnp.float32)

    @pl.when(step == pl.num_programs(0) - 1)
    def _():
        for j in range(exp_local):
            hidden = (jax.nn.silu(gate_acc[j]) * up_acc[j]).astype(jnp.bfloat16)
            out_ref[:, j] = hidden.reshape(4 * each, slots, hidden.shape[-1])


def gate_up(ids, q_in, parts, gate_weight, up_weight, slots):
    _, exp_local, tok = q_in.shape
    _, width_all, hid = gate_weight.shape
    count = 4 * parts[0].shape[0] // tok
    wide = width_all // STEPS
    weight_spec = pl.BlockSpec((exp_local, wide, hid), lambda k, ids: (0, k, 0))
    part_spec = pl.BlockSpec((parts[0].shape[0], wide), lambda k, ids: (0, k))
    flops = 2 * exp_local * count * slots * width_all * 2 * hid
    return pl.pallas_call(
        lambda *refs: gate_up_body(slots, *refs),
        out_shape=jax.ShapeDtypeStruct((count, exp_local, slots, hid), jnp.bfloat16),
        grid_spec=pltpu.PrefetchScalarGridSpec(
            num_scalar_prefetch=1,
            grid=(STEPS,),
            in_specs=[
                pl.BlockSpec(q_in.shape, lambda k, ids: (0, 0, 0)),
                *[part_spec] * 4,
                weight_spec,
                weight_spec,
            ],
            out_specs=pl.BlockSpec((count, exp_local, slots, hid), lambda k, ids: (0, 0, 0, 0)),
            scratch_shapes=[
                pltpu.VMEM((exp_local, count * slots, wide), jnp.bfloat16),
                pltpu.VMEM((exp_local, count * slots, hid), jnp.float32),
                pltpu.VMEM((exp_local, count * slots, hid), jnp.float32),
            ],
        ),
        compiler_params=pltpu.CompilerParams(vmem_limit_bytes=VMEM_BYTES),
        cost_estimate=pl.CostEstimate(
            flops=flops,
            transcendentals=0,
            bytes_accessed=2 * (2 * exp_local * width_all * hid + count * tok * width_all),
        ),
        name="gate_up",
    )(ids, q_in, *parts, gate_weight, up_weight)


def down_body(chunks, ids_ref, *refs):
    hs = refs[: 4 * chunks]
    ws = refs[4 * chunks : 4 * chunks + 4]
    out_ref, rows_ref, sem = refs[-3:]
    count, exp_local, slots, hid = hs[0].shape
    cols = ws[0].shape[-1]
    copies = []
    for n in range(chunks):
        for j in range(exp_local):
            total = jnp.zeros((count * slots, cols), jnp.float32)
            for y in range(4):
                total = total + jnp.dot(
                    hs[4 * n + y][:, j].reshape(count * slots, hid),
                    ws[y][j],
                    preferred_element_type=jnp.float32,
                )
            rows_ref[n, :, j] = total.astype(jnp.bfloat16).reshape(count, slots, cols)
        for b in range(count):
            copy = pltpu.make_async_copy(
                rows_ref.at[n, b], out_ref.at[ids_ref[n * count + b]], sem.at[n * count + b]
            )
            copy.start()
            copies.append(copy)
    for copy in copies:
        copy.wait()


def down(ids, hidden, weights, sources, before=None):
    chunks = len(hidden)
    count, exp_local, slots, hid = hidden[0][0].shape
    cols = weights[0].shape[-1]
    flat = [h for four in hidden for h in four]
    operands = [ids, *flat, *weights]
    specs = [pl.BlockSpec(memory_space=pltpu.VMEM)] * (len(flat) + 4)
    aliases = {}
    if before is not None:
        aliases = {len(operands): 0}
        operands.append(before)
        specs = specs + [pl.BlockSpec(memory_space=pl.ANY)]
    return pl.pallas_call(
        lambda *refs: down_body(chunks, *refs),
        out_shape=jax.ShapeDtypeStruct((sources, exp_local, slots, cols), jnp.bfloat16),
        grid_spec=pltpu.PrefetchScalarGridSpec(
            num_scalar_prefetch=1,
            grid=(),
            in_specs=specs,
            out_specs=pl.BlockSpec(memory_space=pl.ANY),
            scratch_shapes=[
                pltpu.VMEM((chunks, count, exp_local, slots, cols), jnp.bfloat16),
                pltpu.SemaphoreType.DMA((chunks * count,)),
            ],
        ),
        input_output_aliases=aliases,
        compiler_params=pltpu.CompilerParams(vmem_limit_bytes=VMEM_BYTES),
        cost_estimate=pl.CostEstimate(
            flops=2 * chunks * exp_local * count * slots * cols * 4 * hid,
            transcendentals=0,
            bytes_accessed=2 * (exp_local * 4 * hid * cols + chunks * exp_local * count * slots * cols),
        ),
        name="down",
    )(*operands)


def place_of(z, x, c):
    return (z % SIDE) * SIDE * 2 + (x % SIDE) * 2 + c


def move(axis, by):
    pairs = []
    for z in range(SIDE):
        for x in range(SIDE):
            for c in range(2):
                along_z = (axis == 0) == (c == 0)
                to = place_of(z + by, x, c) if along_z else place_of(z, x + by, c)
                pairs.append((place_of(z, x, c), to))
    return pairs


def other_core():
    spots = [(z, x, c) for z in range(SIDE) for x in range(SIDE) for c in range(2)]
    return [(place_of(z, x, c), place_of(z, x, 1 - c)) for z, x, c in spots]


def gather_chunks(tokens):
    half = tokens.shape[0] // 2
    send = lambda v, axis, by: lax.ppermute(v, "expert", move(axis, by))
    swap = lambda v: lax.ppermute(v, "expert", other_core())
    fore, back = send(tokens, 0, 1), send(tokens, 0, -1)
    far = [send(fore[:half], 0, 1), send(back[half:], 0, -1)]
    near_a = jnp.concatenate([tokens, fore], axis=0)
    near_b = jnp.concatenate([back, *far], axis=0)
    fore_a, back_b = send(near_a, 1, 1), send(near_b, 1, -1)
    fore_b, back_a = send(near_b, 1, 1), send(near_a, 1, -1)
    far_a, far_b = send(fore_a, 1, 1), send(back_b, 1, -1)
    pairs = [(near_a, near_b), (fore_a, back_b), (fore_b, back_a), (far_a, far_b)]
    return [[a, swap(a), b, swap(b)] for a, b in pairs]


def chunk_ids():
    me = lax.axis_index("expert")
    z, x, c = me // (2 * SIDE), me // 2 % SIDE, me % 2
    near, wide = (0, -1), (1, 2)
    chunks = [
        ((near, 0), (wide, 0)),
        ((near, -1), (wide, 1)),
        ((wide, -1), (near, 1)),
        ((near, -2), (wide, 2)),
    ]
    first, second, kinds = [], [], []
    for halves in chunks:
        for along, across in halves:
            for kind in (0, 1):
                for step in along:
                    first.append(step)
                    second.append(across)
                    kinds.append(kind)
    first, second, kinds = (jnp.array(v, jnp.int32) for v in (first, second, kinds))
    core = jnp.where(kinds == 0, c, 1 - c)
    dz = jnp.where(core == 0, first, second)
    dx = jnp.where(core == 0, second, first)
    ids = (z + dz + SIDE) % SIDE * (2 * SIDE) + (x + dx + SIDE) % SIDE * 2 + core
    return ids.astype(jnp.int32).reshape(4, -1)


def around(v, by):
    n = lax.axis_size("width")
    return lax.ppermute(v, "width", [(i, (i + by) % n) for i in range(n)])


def local(tokens, expert_ids, combine_weights, gate_weight, up_weight, down_weight):
    tok_rows = tokens.shape[0]
    exp_local = gate_weight.shape[0]
    n_expert = lax.axis_size("expert")
    n_width = lax.axis_size("width")
    experts_all = exp_local * n_expert
    slots = min(MOST, tok_rows)

    experts = jnp.arange(experts_all, dtype=jnp.int32)
    hit = expert_ids.T[:, None, :] == experts[None, :, None]
    member = jnp.any(hit, axis=0)
    weight_of = jnp.sum(jnp.where(hit, combine_weights.T[:, None, :], 0.0), axis=0)
    order = jnp.arange(tok_rows, dtype=jnp.int32)
    earlier = (order[:, None] < order[None, :]).astype(jnp.bfloat16)
    rank = jnp.dot(member.astype(jnp.bfloat16), earlier, preferred_element_type=jnp.float32)
    place = jnp.where(member, rank.astype(jnp.int32), -1)
    q_in = lax.all_to_all(
        place.reshape(n_expert, exp_local, tok_rows), "expert", split_axis=0, concat_axis=0, tiled=True
    )
    seat = place[:, None, :] == jnp.arange(slots, dtype=jnp.int32)[None, :, None]
    spread = jnp.where(seat, weight_of[:, None, :], 0.0).reshape(experts_all * slots, tok_rows)
    high = spread.astype(jnp.bfloat16)
    low = (spread - high.astype(jnp.float32)).astype(jnp.bfloat16)

    cols = down_weight.shape[2] // n_width
    mine = lax.axis_index("width")
    cut = lambda by: lax.dynamic_slice_in_dim(down_weight, (mine + by) % n_width * cols, cols, 2)
    weights = [cut(0), around(cut(1), 1), around(cut(3), -1), around(cut(2), 2)]

    ids = chunk_ids()
    hidden = []
    for n, parts in enumerate(gather_chunks(tokens)):
        h = gate_up(ids[n], q_in, parts, gate_weight, up_weight, slots)
        half = h.shape[0] // 2
        fore, back = around(h, 1), around(h, -1)
        far = jnp.concatenate([around(fore[:half], 1), around(back[half:], -1)], axis=0)
        hidden.append([h, fore, back, far])
    rows = down(ids[:3].reshape(-1), hidden[:3], weights, n_expert)
    rows = down(ids[3], hidden[3:], weights, n_expert, rows)

    returned = lax.all_to_all(rows, "expert", split_axis=0, concat_axis=0, tiled=True)
    returned = returned.reshape(experts_all * slots, cols)
    both = jnp.concatenate([high, low], axis=1)
    mixed = lax.dot_general(
        both, returned, (((0,), (0,)), ((), ())), preferred_element_type=jnp.float32
    )
    return (mixed[:tok_rows] + mixed[tok_rows:]).astype(jnp.bfloat16)


def solution(mesh):
    placed = (
        P("expert", None),
        P("expert", None),
        P("expert", None),
        P("expert", None, "width"),
        P("expert", None, "width"),
        P("expert", "width", None),
    )
    return jax.shard_map(
        local, mesh=mesh, in_specs=placed, out_specs=P("expert", "width"), check_vma=False
    )
```

```python
import jax
import jax.numpy as jnp
from jax import lax
from jax.experimental import pallas as pl
from jax.experimental.pallas import tpu as pltpu
from jax.sharding import PartitionSpec as P

MOST = 32
VMEM_BYTES = 60 * 1024 * 1024


def gate_up_body(group, slots, j, x_ref, q_ref, gate_ref, up_ref, out_ref, rows_ref):
    tok = x_ref.shape[0] // group
    width_all = x_ref.shape[1]
    place = lax.broadcasted_iota(jnp.int32, (slots, tok), 0)
    for b in range(group):
        pick = jnp.where(place == q_ref[b, j][None, :], 1.0, 0.0).astype(jnp.bfloat16)
        for c in range(0, width_all, 1024):
            rows_ref[b * slots : (b + 1) * slots, c : c + 1024] = jnp.dot(
                pick,
                x_ref[b * tok : (b + 1) * tok, c : c + 1024],
                preferred_element_type=jnp.float32,
            ).astype(jnp.bfloat16)
    hid = gate_ref.shape[-1]
    joined = jnp.concatenate([gate_ref[0], up_ref[0]], axis=1)
    both = jnp.dot(rows_ref[...], joined, preferred_element_type=jnp.float32)
    hidden = (jax.nn.silu(both[:, :hid]) * both[:, hid:]).astype(jnp.bfloat16)
    out_ref[...] = hidden.reshape(group, slots, hid)


def gate_up(x_all, q_in, gate_weight, up_weight, slots, j, group=8):
    sources, exp_local, tok = q_in.shape
    _, width_all, hid = gate_weight.shape
    weight_spec = pl.BlockSpec(
        (1, width_all, hid), lambda i: (j, 0, 0), pipeline_mode=pl.Buffered(1)
    )
    return pl.pallas_call(
        lambda *refs: gate_up_body(group, slots, j, *refs),
        out_shape=jax.ShapeDtypeStruct((sources, slots, hid), jnp.bfloat16),
        grid=(sources // group,),
        in_specs=[
            pl.BlockSpec((group * tok, width_all), lambda i: (i, 0)),
            pl.BlockSpec((group, exp_local, tok), lambda i: (i, 0, 0)),
            weight_spec,
            weight_spec,
        ],
        out_specs=pl.BlockSpec((group, slots, hid), lambda i: (i, 0, 0)),
        scratch_shapes=[pltpu.VMEM((group * slots, width_all), jnp.bfloat16)],
        compiler_params=pltpu.CompilerParams(vmem_limit_bytes=VMEM_BYTES),
        cost_estimate=pl.CostEstimate(
            flops=4 * sources * slots * width_all * hid,
            transcendentals=0,
            bytes_accessed=2 * (sources * tok * width_all + 2 * width_all * hid),
        ),
        name="gate_up",
    )(x_all, q_in, gate_weight, up_weight)


def down_body(*refs):
    hs, ws, out_ref = refs[:4], refs[4:8], refs[8]
    group, slots, hid = hs[0].shape
    rows = jnp.concatenate([h[...].reshape(group * slots, hid) for h in hs], axis=1)
    weight = jnp.concatenate([w[0] for w in ws], axis=0)
    total = jnp.dot(rows, weight, preferred_element_type=jnp.float32)
    out_ref[...] = total.astype(jnp.bfloat16).reshape(out_ref.shape)


def down(hidden, weights, j, group=8):
    sources, slots, hid = hidden[0].shape
    cols = weights[0].shape[-1]
    return pl.pallas_call(
        down_body,
        out_shape=jax.ShapeDtypeStruct((sources, slots, cols), jnp.bfloat16),
        grid=(sources // group,),
        in_specs=[pl.BlockSpec((group, slots, hid), lambda i: (i, 0, 0))] * 4
        + [pl.BlockSpec((1, hid, cols), lambda i: (j, 0, 0), pipeline_mode=pl.Buffered(1))] * 4,
        out_specs=pl.BlockSpec((group, slots, cols), lambda i: (i, 0, 0)),
        compiler_params=pltpu.CompilerParams(vmem_limit_bytes=VMEM_BYTES),
        cost_estimate=pl.CostEstimate(
            flops=8 * sources * slots * hid * cols,
            transcendentals=0,
            bytes_accessed=2 * (4 * sources * slots * hid + 4 * hid * cols + sources * slots * cols),
        ),
        name="down",
    )(*hidden, *weights)


def around(v, by):
    n = lax.axis_size("width")
    return lax.ppermute(v, "width", [(i, (i + by) % n) for i in range(n)])


def local(tokens, expert_ids, combine_weights, gate_weight, up_weight, down_weight):
    tok_rows = tokens.shape[0]
    exp_local = gate_weight.shape[0]
    n_expert = lax.axis_size("expert")
    experts_all = exp_local * n_expert
    slots = min(MOST, tok_rows)

    x_all = lax.all_gather(tokens, "expert", axis=0, tiled=True)

    experts = jnp.arange(experts_all, dtype=jnp.int32)
    hit = expert_ids.T[:, None, :] == experts[None, :, None]
    member = jnp.any(hit, axis=0)
    weight_of = jnp.sum(jnp.where(hit, combine_weights.T[:, None, :], 0.0), axis=0)
    order = jnp.arange(tok_rows, dtype=jnp.int32)
    earlier = (order[:, None] < order[None, :]).astype(jnp.bfloat16)
    rank = jnp.dot(member.astype(jnp.bfloat16), earlier, preferred_element_type=jnp.float32)
    place = jnp.where(member, rank.astype(jnp.int32), -1)
    q_in = lax.all_to_all(
        place.reshape(n_expert, exp_local, tok_rows), "expert", split_axis=0, concat_axis=0, tiled=True
    )
    seat = place[:, None, :] == jnp.arange(slots, dtype=jnp.int32)[None, :, None]
    spread = jnp.where(seat, weight_of[:, None, :], 0.0)
    spread = spread.reshape(n_expert, exp_local, slots, tok_rows)
    high = spread.astype(jnp.bfloat16)
    low = (spread - high.astype(jnp.float32)).astype(jnp.bfloat16)
    seats = jnp.concatenate([high, low], axis=3)

    n_width = lax.axis_size("width")
    cols = down_weight.shape[2] // n_width
    mine = lax.axis_index("width")
    cut = lambda by: lax.dynamic_slice_in_dim(down_weight, (mine + by) % n_width * cols, cols, 2)
    weights = [cut(0), around(cut(1), 1), around(cut(3), -1), around(cut(2), 2)]
    x_all, q_in, seats, *weights = lax.optimization_barrier((x_all, q_in, seats, *weights))

    mixed = jnp.zeros((2 * tok_rows, cols), jnp.float32)
    hidden = [gate_up(x_all, q_in, gate_weight, up_weight, slots, j) for j in range(exp_local)]
    rings = [[h, around(h, 1), around(h, -1), around(h, 2)] for h in hidden]
    rings[0], hidden[-1] = lax.optimization_barrier((rings[0], hidden[-1]))
    rings[-1][0] = hidden[-1]
    for j, ring in enumerate(rings):
        rows = down(ring, weights, j)
        returned = lax.all_to_all(rows, "expert", split_axis=0, concat_axis=0, tiled=True)
        mixed = mixed + lax.dot_general(
            seats[:, j].reshape(n_expert * slots, 2 * tok_rows),
            returned.reshape(n_expert * slots, cols),
            (((0,), (0,)), ((), ())),
            preferred_element_type=jnp.float32,
        )
    return (mixed[:tok_rows] + mixed[tok_rows:]).astype(jnp.bfloat16)


def solution(mesh):
    placed = (
        P("expert", None),
        P("expert", None),
        P("expert", None),
        P("expert", None, "width"),
        P("expert", None, "width"),
        P("expert", "width", None),
    )
    return jax.shard_map(
        local, mesh=mesh, in_specs=placed, out_specs=P("expert", "width"), check_vma=False
    )
```

```python
import jax
import jax.numpy as jnp
from jax import lax
from jax.experimental import pallas as pl
from jax.experimental.pallas import tpu as pltpu
from jax.sharding import PartitionSpec as P

MOST = 32
VMEM_BYTES = 60 * 1024 * 1024


def gate_up_body(group, slots, j, x_ref, q_ref, gate_ref, up_ref, out_ref, rows_ref):
    tok = x_ref.shape[0] // group
    width_all = x_ref.shape[1]
    place = lax.broadcasted_iota(jnp.int32, (slots, tok), 0)
    for b in range(group):
        pick = jnp.where(place == q_ref[b, j][None, :], 1.0, 0.0).astype(jnp.bfloat16)
        for c in range(0, width_all, 1024):
            rows_ref[b * slots : (b + 1) * slots, c : c + 1024] = jnp.dot(
                pick,
                x_ref[b * tok : (b + 1) * tok, c : c + 1024],
                preferred_element_type=jnp.float32,
            ).astype(jnp.bfloat16)
    hid = gate_ref.shape[-1]
    joined = jnp.concatenate([gate_ref[0], up_ref[0]], axis=1)
    both = jnp.dot(rows_ref[...], joined, preferred_element_type=jnp.float32)
    hidden = (jax.nn.silu(both[:, :hid]) * both[:, hid:]).astype(jnp.bfloat16)
    out_ref[...] = hidden.reshape(group, slots, hid)


def gate_up(x_all, q_in, gate_weight, up_weight, slots, j, group=8):
    sources, exp_local, tok = q_in.shape
    _, width_all, hid = gate_weight.shape
    weight_spec = pl.BlockSpec(
        (1, width_all, hid), lambda i: (j, 0, 0), pipeline_mode=pl.Buffered(1)
    )
    return pl.pallas_call(
        lambda *refs: gate_up_body(group, slots, j, *refs),
        out_shape=jax.ShapeDtypeStruct((sources, slots, hid), jnp.bfloat16),
        grid=(sources // group,),
        in_specs=[
            pl.BlockSpec((group * tok, width_all), lambda i: (i, 0)),
            pl.BlockSpec((group, exp_local, tok), lambda i: (i, 0, 0)),
            weight_spec,
            weight_spec,
        ],
        out_specs=pl.BlockSpec((group, slots, hid), lambda i: (i, 0, 0)),
        scratch_shapes=[pltpu.VMEM((group * slots, width_all), jnp.bfloat16)],
        compiler_params=pltpu.CompilerParams(vmem_limit_bytes=VMEM_BYTES),
        cost_estimate=pl.CostEstimate(
            flops=4 * sources * slots * width_all * hid,
            transcendentals=0,
            bytes_accessed=2 * (sources * tok * width_all + 2 * width_all * hid),
        ),
        name="gate_up",
    )(x_all, q_in, gate_weight, up_weight)


def down_body(half_steps, *refs):
    hs, far, ws, out_ref, far_ref = refs[:3], refs[3:5], refs[5:9], refs[9], refs[10]
    group, slots, hid = hs[0].shape

    @pl.when(pl.program_id(0) < half_steps)
    def _():
        far_ref[...] = far[0][...]

    @pl.when(pl.program_id(0) >= half_steps)
    def _():
        far_ref[...] = far[1][...]

    rows = jnp.concatenate(
        [h[...].reshape(group * slots, hid) for h in (*hs, far_ref)], axis=1
    )
    weight = jnp.concatenate([w[0] for w in ws], axis=0)
    total = jnp.dot(rows, weight, preferred_element_type=jnp.float32)
    out_ref[...] = total.astype(jnp.bfloat16).reshape(out_ref.shape)


def down(ring, weights, j, group=8):
    own, fore, back, (far_low, far_high) = ring
    sources, slots, hid = own.shape
    cols = weights[0].shape[-1]
    steps = sources // group
    half = steps // 2
    low_at = far_low.shape[0] // group - half
    high_at = far_high.shape[0] // group - half
    spec = pl.BlockSpec((group, slots, hid), lambda i: (i, 0, 0))
    low_spec = pl.BlockSpec(
        (group, slots, hid), lambda i: (low_at + jnp.minimum(i, half - 1), 0, 0)
    )
    high_spec = pl.BlockSpec(
        (group, slots, hid), lambda i: (high_at + jnp.maximum(i - half, 0), 0, 0)
    )
    return pl.pallas_call(
        lambda *refs: down_body(half, *refs),
        out_shape=jax.ShapeDtypeStruct((sources, slots, cols), jnp.bfloat16),
        grid=(steps,),
        in_specs=[spec] * 3
        + [low_spec, high_spec]
        + [pl.BlockSpec((1, hid, cols), lambda i: (j, 0, 0), pipeline_mode=pl.Buffered(1))] * 4,
        out_specs=pl.BlockSpec((group, slots, cols), lambda i: (i, 0, 0)),
        scratch_shapes=[pltpu.VMEM((group, slots, hid), jnp.bfloat16)],
        compiler_params=pltpu.CompilerParams(vmem_limit_bytes=VMEM_BYTES),
        cost_estimate=pl.CostEstimate(
            flops=8 * sources * slots * hid * cols,
            transcendentals=0,
            bytes_accessed=2 * (4 * sources * slots * hid + 4 * hid * cols + sources * slots * cols),
        ),
        name="down",
    )(own, fore, back, far_low, far_high, *weights)


def around(v, by):
    n = lax.axis_size("width")
    return lax.ppermute(v, "width", [(i, (i + by) % n) for i in range(n)])


def local(tokens, expert_ids, combine_weights, gate_weight, up_weight, down_weight):
    tok_rows = tokens.shape[0]
    exp_local = gate_weight.shape[0]
    n_expert = lax.axis_size("expert")
    experts_all = exp_local * n_expert
    slots = min(MOST, tok_rows)

    x_all = lax.all_gather(tokens, "expert", axis=0, tiled=True)

    experts = jnp.arange(experts_all, dtype=jnp.int32)
    hit = expert_ids.T[:, None, :] == experts[None, :, None]
    member = jnp.any(hit, axis=0)
    weight_of = jnp.sum(jnp.where(hit, combine_weights.T[:, None, :], 0.0), axis=0)
    order = jnp.arange(tok_rows, dtype=jnp.int32)
    earlier = (order[:, None] < order[None, :]).astype(jnp.bfloat16)
    rank = jnp.dot(member.astype(jnp.bfloat16), earlier, preferred_element_type=jnp.float32)
    place = jnp.where(member, rank.astype(jnp.int32), -1)
    q_in = lax.all_to_all(
        place.reshape(n_expert, exp_local, tok_rows), "expert", split_axis=0, concat_axis=0, tiled=True
    )
    seat = place[:, None, :] == jnp.arange(slots, dtype=jnp.int32)[None, :, None]
    spread = jnp.where(seat, weight_of[:, None, :], 0.0)
    spread = spread.reshape(n_expert, exp_local, slots, tok_rows)
    high = spread.astype(jnp.bfloat16)
    low = (spread - high.astype(jnp.float32)).astype(jnp.bfloat16)
    seats = jnp.concatenate([high, low], axis=3)

    n_width = lax.axis_size("width")
    cols = down_weight.shape[2] // n_width
    mine = lax.axis_index("width")
    cut = lambda by: lax.dynamic_slice_in_dim(down_weight, (mine + by) % n_width * cols, cols, 2)
    weights = [cut(0), around(cut(1), 1), around(cut(3), -1), around(cut(2), 2)]
    x_all, q_in, seats, *weights = lax.optimization_barrier((x_all, q_in, seats, *weights))

    mixed = jnp.zeros((2 * tok_rows, cols), jnp.float32)
    hidden = [gate_up(x_all, q_in, gate_weight, up_weight, slots, j) for j in range(exp_local)]
    half = n_expert // 2
    first, last = hidden
    fore, back = around(first, 1), around(first, -1)
    fore, back, last = lax.optimization_barrier((fore, back, last))
    ahead = around(jnp.concatenate([last, fore[:half]], axis=0), 1)
    behind = around(jnp.concatenate([last, back[half:]], axis=0), -1)
    rings = [[first, fore, back, (ahead, behind)]]
    rings.append([last, ahead, behind, (around(ahead[:half], 1), around(behind[half:n_expert], -1))])
    for j, ring in enumerate(rings):
        rows = down(ring, weights, j)
        returned = lax.all_to_all(rows, "expert", split_axis=0, concat_axis=0, tiled=True)
        mixed = mixed + lax.dot_general(
            seats[:, j].reshape(n_expert * slots, 2 * tok_rows),
            returned.reshape(n_expert * slots, cols),
            (((0,), (0,)), ((), ())),
            preferred_element_type=jnp.float32,
        )
    return (mixed[:tok_rows] + mixed[tok_rows:]).astype(jnp.bfloat16)


def solution(mesh):
    placed = (
        P("expert", None),
        P("expert", None),
        P("expert", None),
        P("expert", None, "width"),
        P("expert", None, "width"),
        P("expert", "width", None),
    )
    return jax.shard_map(
        local, mesh=mesh, in_specs=placed, out_specs=P("expert", "width"), check_vma=False
    )
```

```python
import jax
import jax.numpy as jnp
from jax import lax
from jax.experimental import pallas as pl
from jax.experimental.pallas import tpu as pltpu
from jax.sharding import PartitionSpec as P

MOST = 32
SIDE = 4
STEPS = 4
VMEM_BYTES = 56 * 1024 * 1024


def gate_up_body(slots, ids_ref, q_ref, *refs):
    parts = refs[:4]
    gate_ref, up_ref, out_ref, rows_ref, acc_ref = refs[4:]
    step = pl.program_id(0)
    tok = q_ref.shape[-1]
    exp_local = gate_ref.shape[0]
    each = parts[0].shape[0] // tok
    place = lax.broadcasted_iota(jnp.int32, (slots, tok), 0)

    @pl.when(step == 0)
    def _():
        acc_ref[...] = jnp.zeros_like(acc_ref)

    for b in range(4 * each):
        seats = q_ref[ids_ref[b]]
        pick = jnp.concatenate(
            [
                jnp.where(place == seats[j][None, :], 1.0, 0.0).astype(jnp.bfloat16)
                for j in range(exp_local)
            ],
            axis=0,
        )
        at = (b % each) * tok
        rows = jnp.dot(
            pick, parts[b // each][at : at + tok, :], preferred_element_type=jnp.float32
        ).astype(jnp.bfloat16)
        for j in range(exp_local):
            rows_ref[j, b * slots : (b + 1) * slots, :] = rows[j * slots : (j + 1) * slots]
    for j in range(exp_local):
        joined = jnp.concatenate([gate_ref[j], up_ref[j]], axis=1)
        acc_ref[j] += jnp.dot(rows_ref[j], joined, preferred_element_type=jnp.float32)

    @pl.when(step == pl.num_programs(0) - 1)
    def _():
        for j in range(exp_local):
            hid = gate_ref.shape[-1]
            hidden = (jax.nn.silu(acc_ref[j, :, :hid]) * acc_ref[j, :, hid:]).astype(jnp.bfloat16)
            out_ref[:, j] = hidden.reshape(4 * each, slots, hid)


def gate_up(ids, q_in, parts, gate_weight, up_weight, slots):
    _, exp_local, tok = q_in.shape
    _, width_all, hid = gate_weight.shape
    count = 4 * parts[0].shape[0] // tok
    wide = width_all // STEPS
    weight_spec = pl.BlockSpec((exp_local, wide, hid), lambda k, ids: (0, k, 0))
    part_spec = pl.BlockSpec((parts[0].shape[0], wide), lambda k, ids: (0, k))
    return pl.pallas_call(
        lambda *refs: gate_up_body(slots, *refs),
        out_shape=jax.ShapeDtypeStruct((count, exp_local, slots, hid), jnp.bfloat16),
        grid_spec=pltpu.PrefetchScalarGridSpec(
            num_scalar_prefetch=1,
            grid=(STEPS,),
            in_specs=[
                pl.BlockSpec(q_in.shape, lambda k, ids: (0, 0, 0)),
                *[part_spec] * 4,
                weight_spec,
                weight_spec,
            ],
            out_specs=pl.BlockSpec((count, exp_local, slots, hid), lambda k, ids: (0, 0, 0, 0)),
            scratch_shapes=[
                pltpu.VMEM((exp_local, count * slots, wide), jnp.bfloat16),
                pltpu.VMEM((exp_local, count * slots, 2 * hid), jnp.float32),
            ],
        ),
        compiler_params=pltpu.CompilerParams(vmem_limit_bytes=VMEM_BYTES),
        cost_estimate=pl.CostEstimate(flops=1, transcendentals=0, bytes_accessed=1),
        name="gate_up",
    )(ids, q_in, *parts, gate_weight, up_weight)


def down_body(chunks, ids_ref, *refs):
    hs, w_ref = refs[:chunks], refs[chunks]
    out_ref, rows_ref, sem = refs[-3:]
    n_width, count, exp_local, slots, hid = hs[0].shape
    cols = w_ref.shape[-1]
    copies = []
    for n in range(chunks):
        for j in range(exp_local):
            rows = [hs[n][y, :, j].reshape(count * slots, hid) for y in range(n_width)]
            weight = [w_ref[y, j] for y in range(n_width)]
            total = jnp.dot(
                jnp.concatenate(rows, axis=1),
                jnp.concatenate(weight, axis=0),
                preferred_element_type=jnp.float32,
            )
            rows_ref[n, :, j] = total.astype(jnp.bfloat16).reshape(count, slots, cols)
        for b in range(count):
            copy = pltpu.make_async_copy(
                rows_ref.at[n, b], out_ref.at[ids_ref[n * count + b]], sem.at[n * count + b]
            )
            copy.start()
            copies.append(copy)
    for copy in copies:
        copy.wait()


def down(ids, hidden, weights, sources, before=None):
    chunks = len(hidden)
    _, count, exp_local, slots, hid = hidden[0].shape
    cols = weights.shape[-1]
    operands = [ids, *hidden, weights]
    specs = [pl.BlockSpec(memory_space=pltpu.VMEM)] * (chunks + 1)
    aliases = {}
    if before is not None:
        aliases = {len(operands): 0}
        operands.append(before)
        specs = specs + [pl.BlockSpec(memory_space=pl.ANY)]
    return pl.pallas_call(
        lambda *refs: down_body(chunks, *refs),
        out_shape=jax.ShapeDtypeStruct((sources, exp_local, slots, cols), jnp.bfloat16),
        grid_spec=pltpu.PrefetchScalarGridSpec(
            num_scalar_prefetch=1,
            grid=(),
            in_specs=specs,
            out_specs=pl.BlockSpec(memory_space=pl.ANY),
            scratch_shapes=[
                pltpu.VMEM((chunks, count, exp_local, slots, cols), jnp.bfloat16),
                pltpu.SemaphoreType.DMA((chunks * count,)),
            ],
        ),
        input_output_aliases=aliases,
        compiler_params=pltpu.CompilerParams(vmem_limit_bytes=VMEM_BYTES),
        cost_estimate=pl.CostEstimate(flops=1, transcendentals=0, bytes_accessed=1),
        name="down",
    )(*operands)


def place_of(z, x, c):
    return (z % SIDE) * SIDE * 2 + (x % SIDE) * 2 + c


def move(axis, by):
    pairs = []
    for z in range(SIDE):
        for x in range(SIDE):
            for c in range(2):
                along_z = (axis == 0) == (c == 0)
                to = place_of(z + by, x, c) if along_z else place_of(z, x + by, c)
                pairs.append((place_of(z, x, c), to))
    return pairs


def other_core():
    spots = [(z, x, c) for z in range(SIDE) for x in range(SIDE) for c in range(2)]
    return [(place_of(z, x, c), place_of(z, x, 1 - c)) for z, x, c in spots]


def gather_chunks(tokens, q_in, weights):
    half = tokens.shape[0] // 2
    send = lambda v, axis, by: lax.ppermute(v, "expert", move(axis, by))
    swap = lambda v: lax.ppermute(v, "expert", other_core())
    fore, back = send(tokens, 0, 1), send(tokens, 0, -1)
    fore, back = lax.optimization_barrier((fore, back))
    far = [send(fore[:half], 0, 1), send(back[half:], 0, -1)]
    near_a = jnp.concatenate([tokens, fore], axis=0)
    near_b = jnp.concatenate([back, *far], axis=0)
    fore_a, back_a = send(near_a, 1, 1), send(near_a, 1, -1)
    fore_b, back_b = send(near_b, 1, 1), send(near_b, 1, -1)
    back_b, weights = lax.optimization_barrier((back_b, weights))
    far_a, far_b = send(fore_a, 1, 1), send(back_b, 1, -1)
    pairs = [(near_a, near_b), (fore_a, back_a), (fore_b, back_b), (far_a, far_b)]
    return [[a, swap(a), b, swap(b)] for a, b in pairs], q_in, weights


def chunk_ids():
    me = lax.axis_index("expert")
    z, x, c = me // (2 * SIDE), me // 2 % SIDE, me % 2
    near, wide = (0, -1), (1, 2)
    chunks = [
        ((near, 0), (wide, 0)),
        ((near, -1), (near, 1)),
        ((wide, -1), (wide, 1)),
        ((near, -2), (wide, 2)),
    ]
    first, second, kinds = [], [], []
    for halves in chunks:
        for along, across in halves:
            for kind in (0, 1):
                for step in along:
                    first.append(step)
                    second.append(across)
                    kinds.append(kind)
    first, second, kinds = (jnp.array(v, jnp.int32) for v in (first, second, kinds))
    core = jnp.where(kinds == 0, c, 1 - c)
    dz = jnp.where(core == 0, first, second)
    dx = jnp.where(core == 0, second, first)
    ids = (z + dz + SIDE) % SIDE * (2 * SIDE) + (x + dx + SIDE) % SIDE * 2 + core
    return ids.astype(jnp.int32).reshape(4, -1)


def local(tokens, expert_ids, combine_weights, gate_weight, up_weight, down_weight):
    tok_rows = tokens.shape[0]
    exp_local = gate_weight.shape[0]
    n_expert = lax.axis_size("expert")
    n_width = lax.axis_size("width")
    experts_all = exp_local * n_expert
    slots = min(MOST, tok_rows)

    experts = jnp.arange(experts_all, dtype=jnp.int32)
    hit = expert_ids.T[:, None, :] == experts[None, :, None]
    member = jnp.any(hit, axis=0)
    weight_of = jnp.sum(jnp.where(hit, combine_weights.T[:, None, :], 0.0), axis=0)
    order = jnp.arange(tok_rows, dtype=jnp.int32)
    earlier = (order[:, None] < order[None, :]).astype(jnp.bfloat16)
    rank = jnp.dot(member.astype(jnp.bfloat16), earlier, preferred_element_type=jnp.float32)
    place = jnp.where(member, rank.astype(jnp.int32), -1)
    q_all = lax.all_gather(place, "expert", axis=0, tiled=False)
    q_in = lax.dynamic_slice_in_dim(q_all, lax.axis_index("expert") * exp_local, exp_local, 1)
    seat = place[:, None, :] == jnp.arange(slots, dtype=jnp.int32)[None, :, None]
    spread = jnp.where(seat, weight_of[:, None, :], 0.0).reshape(experts_all * slots, tok_rows)
    high = spread.astype(jnp.bfloat16)
    low = (spread - high.astype(jnp.float32)).astype(jnp.bfloat16)

    cols = down_weight.shape[2] // n_width
    cut = jnp.stack([down_weight[:, :, n * cols : (n + 1) * cols] for n in range(n_width)])
    weights = lax.all_to_all(cut, "width", split_axis=0, concat_axis=0, tiled=True)

    ids = chunk_ids()
    hidden = []
    chunks, q_in, weights = gather_chunks(tokens, q_in, weights)
    for n, parts in enumerate(chunks):
        h = gate_up(ids[n], q_in, parts, gate_weight, up_weight, slots)
        hidden.append(lax.all_gather(h, "width", axis=0, tiled=False))
    rows = down(ids[:3].reshape(-1), hidden[:3], weights, n_expert)
    rows = down(ids[3], hidden[3:], weights, n_expert, rows)

    returned = lax.all_to_all(rows, "expert", split_axis=0, concat_axis=0, tiled=True)
    returned = returned.reshape(experts_all * slots, cols)
    both = jnp.concatenate([high, low], axis=1)
    mixed = lax.dot_general(
        both, returned, (((0,), (0,)), ((), ())), preferred_element_type=jnp.float32
    )
    return (mixed[:tok_rows] + mixed[tok_rows:]).astype(jnp.bfloat16)


def solution(mesh):
    placed = (
        P("expert", None),
        P("expert", None),
        P("expert", None),
        P("expert", None, "width"),
        P("expert", None, "width"),
        P("expert", "width", None),
    )
    return jax.shard_map(
        local, mesh=mesh, in_specs=placed, out_specs=P("expert", "width"), check_vma=False
    )
```

```python
import jax
import jax.numpy as jnp
from jax import lax
from jax.experimental import pallas as pl
from jax.experimental.pallas import tpu as pltpu
from jax.sharding import PartitionSpec as P

MOST = 32
SIDE = 4
STEPS = 4
RING = (0, 3, 1, 2)
MARK = 8
VMEM_BYTES = 56 * 1024 * 1024


def gate_up_body(slots, tok, each, at_ref, *refs):
    parts, marks = refs[:4], refs[4 : 4 + 4 * each]
    gate_ref, up_ref, out_ref, rows_ref, acc_ref = refs[4 + 4 * each :]
    step = pl.program_id(0)
    exp_local = gate_ref.shape[0]
    block = parts[0].shape[0] // each
    place = lax.broadcasted_iota(jnp.int32, (slots, tok), 0)

    @pl.when(step == 0)
    def _():
        acc_ref[...] = jnp.zeros_like(acc_ref)

    for b in range(4 * each):
        mark = marks[b][...].astype(jnp.int32)
        seats = mark[0:1]
        for r in range(1, mark.shape[0]):
            seats = jnp.where(at_ref[0] == r, mark[r : r + 1], seats)
        pick = jnp.concatenate(
            [
                jnp.where(place == seats[:, j * tok : (j + 1) * tok], 1.0, 0.0).astype(
                    jnp.bfloat16
                )
                for j in range(exp_local)
            ],
            axis=0,
        )
        at = (b % each) * block
        rows = jnp.dot(
            pick, parts[b // each][at : at + tok, :], preferred_element_type=jnp.float32
        ).astype(jnp.bfloat16)
        for j in range(exp_local):
            rows_ref[j, b * slots : (b + 1) * slots, :] = rows[j * slots : (j + 1) * slots]
    for j in range(exp_local):
        joined = jnp.concatenate([gate_ref[j], up_ref[j]], axis=1)
        acc_ref[j] += jnp.dot(rows_ref[j], joined, preferred_element_type=jnp.float32)

    @pl.when(step == pl.num_programs(0) - 1)
    def _():
        for j in range(exp_local):
            hid = gate_ref.shape[-1]
            hidden = (jax.nn.silu(acc_ref[j, :, :hid]) * acc_ref[j, :, hid:]).astype(jnp.bfloat16)
            out_ref[:, j] = hidden.reshape(4 * each, slots, hid)


def gate_up(spot, parts, gate_weight, up_weight, slots, tok):
    exp_local, width_all, hid = gate_weight.shape
    block = tok + MARK
    each = parts[0].shape[0] // block
    count = 4 * each
    wide = width_all // STEPS
    weight_spec = pl.BlockSpec((exp_local, wide, hid), lambda k, at: (0, k, 0))
    part_spec = pl.BlockSpec((parts[0].shape[0], wide), lambda k, at: (0, k))
    mark_specs = [
        pl.BlockSpec(
            (MARK, exp_local * tok),
            lambda k, at, b=b: (b * (block // MARK) + tok // MARK, at[1]),
        )
        for b in range(each)
    ]
    marks = [part for part in parts for _ in range(each)]
    return pl.pallas_call(
        lambda *refs: gate_up_body(slots, tok, each, *refs),
        out_shape=jax.ShapeDtypeStruct((count, exp_local, slots, hid), jnp.bfloat16),
        grid_spec=pltpu.PrefetchScalarGridSpec(
            num_scalar_prefetch=1,
            grid=(STEPS,),
            in_specs=[*[part_spec] * 4, *mark_specs * 4, weight_spec, weight_spec],
        out_specs=pl.BlockSpec((count, exp_local, slots, hid), lambda k, at: (0, 0, 0, 0)),
            scratch_shapes=[
                pltpu.VMEM((exp_local, count * slots, wide), jnp.bfloat16),
                pltpu.VMEM((exp_local, count * slots, 2 * hid), jnp.float32),
            ],
        ),
        compiler_params=pltpu.CompilerParams(vmem_limit_bytes=VMEM_BYTES),
        cost_estimate=pl.CostEstimate(flops=1, transcendentals=0, bytes_accessed=1),
        name="gate_up",
    )(spot, *parts, *marks, gate_weight, up_weight)


def down_body(counts, ids_ref, *refs):
    refs = list(refs)
    out_ref, rows_ref, sem = refs[-3:]
    mine = ids_ref[rows_ref.shape[0]]
    sets = []
    for count in counts:
        sets.append([refs.pop(0)] if count else [refs.pop(0) for _ in RING])
    w_ref = refs[0]
    n_width, exp_local, hid, cols = w_ref.shape
    copies, base = [], 0
    for count, hs in zip(counts, sets):
        blocks, _, slots, _ = hs[0].shape[-4:]
        for j in range(exp_local):
            if count:
                rows = [hs[0][y, :, j].reshape(blocks * slots, hid) for y in range(n_width)]
                weight = [w_ref[y, j] for y in range(n_width)]
            else:
                rows = [h[:, j].reshape(blocks * slots, hid) for h in hs]
                weight = [w_ref[lax.rem(mine + by, n_width), j] for by in RING]
            total = jnp.dot(
                jnp.concatenate(rows, axis=1),
                jnp.concatenate(weight, axis=0),
                preferred_element_type=jnp.float32,
            )
            rows_ref[base : base + blocks, j] = total.astype(jnp.bfloat16).reshape(
                blocks, slots, cols
            )
        for b in range(base, base + blocks):
            copy = pltpu.make_async_copy(rows_ref.at[b], out_ref.at[ids_ref[b]], sem.at[b])
            copy.start()
            copies.append(copy)
        base += blocks
    for copy in copies:
        copy.wait()


def down(ids, hidden, weights, sources, before=None):
    counts = [0 if isinstance(h, list) else h.shape[1] for h in hidden]
    flat = [v for h in hidden for v in (h if isinstance(h, list) else [h])]
    exp_local, slots = flat[0].shape[-3:-1]
    blocks = sum(h[0].shape[0] if isinstance(h, list) else h.shape[1] for h in hidden)
    cols = weights.shape[-1]
    operands = [ids, *flat, weights]
    specs = [pl.BlockSpec(memory_space=pltpu.VMEM)] * (len(flat) + 1)
    aliases = {}
    if before is not None:
        aliases = {len(operands): 0}
        operands.append(before)
        specs = specs + [pl.BlockSpec(memory_space=pl.ANY)]
    return pl.pallas_call(
        lambda *refs: down_body(counts, *refs),
        out_shape=jax.ShapeDtypeStruct((sources, exp_local, slots, cols), jnp.bfloat16),
        grid_spec=pltpu.PrefetchScalarGridSpec(
            num_scalar_prefetch=1,
            grid=(),
            in_specs=specs,
            out_specs=pl.BlockSpec(memory_space=pl.ANY),
            scratch_shapes=[
                pltpu.VMEM((blocks, exp_local, slots, cols), jnp.bfloat16),
                pltpu.SemaphoreType.DMA((blocks,)),
            ],
        ),
        input_output_aliases=aliases,
        compiler_params=pltpu.CompilerParams(vmem_limit_bytes=VMEM_BYTES),
        cost_estimate=pl.CostEstimate(flops=1, transcendentals=0, bytes_accessed=1),
        name="down",
    )(*operands)


def place_of(z, x, c):
    return (z % SIDE) * SIDE * 2 + (x % SIDE) * 2 + c


def move(axis, by):
    pairs = []
    for z in range(SIDE):
        for x in range(SIDE):
            for c in range(2):
                along_z = (axis == 0) == (c == 0)
                to = place_of(z + by, x, c) if along_z else place_of(z, x + by, c)
                pairs.append((place_of(z, x, c), to))
    return pairs


def other_core():
    spots = [(z, x, c) for z in range(SIDE) for x in range(SIDE) for c in range(2)]
    return [(place_of(z, x, c), place_of(z, x, 1 - c)) for z, x, c in spots]


def near_chunks(tokens):
    half = tokens.shape[0] // (2 * MARK) * MARK
    send = lambda v, axis, by: lax.ppermute(v, "expert", move(axis, by))
    fore, back = send(tokens, 0, 1), send(tokens, 0, -1)
    fore, back = lax.optimization_barrier((fore, back))
    far = [send(fore[:half], 0, 1), send(back[half:], 0, -1)]
    near_a = jnp.concatenate([tokens, fore], axis=0)
    near_b = jnp.concatenate([back, *far], axis=0)
    fore_a, back_a = send(near_a, 1, 1), send(near_a, 1, -1)
    fore_b, back_b = send(near_b, 1, 1), send(near_b, 1, -1)
    return (near_a, near_b), (fore_a, back_a), (fore_b, back_b)


def chunk_ids():
    me = lax.axis_index("expert")
    z, x, c = me // (2 * SIDE), me // 2 % SIDE, me % 2
    near, wide = (0, -1), (1, 2)
    chunks = [
        ((near, 0), (wide, 0)),
        ((near, -1), (near, 1)),
        ((wide, -1), (wide, 1)),
        ((near, -2), (wide, 2)),
    ]
    first, second, kinds = [], [], []
    for halves in chunks:
        for along, across in halves:
            for kind in (0, 1):
                for step in along:
                    first.append(step)
                    second.append(across)
                    kinds.append(kind)
    first, second, kinds = (jnp.array(v, jnp.int32) for v in (first, second, kinds))
    core = jnp.where(kinds == 0, c, 1 - c)
    dz = jnp.where(core == 0, first, second)
    dx = jnp.where(core == 0, second, first)
    ids = (z + dz + SIDE) % SIDE * (2 * SIDE) + (x + dx + SIDE) % SIDE * 2 + core
    return ids.astype(jnp.int32).reshape(4, -1)


def around(v, by):
    n = lax.axis_size("width")
    return lax.ppermute(v, "width", [(i, (i + by) % n) for i in range(n)])


def local(tokens, expert_ids, combine_weights, gate_weight, up_weight, down_weight):
    tok_rows = tokens.shape[0]
    exp_local = gate_weight.shape[0]
    n_expert = lax.axis_size("expert")
    n_width = lax.axis_size("width")
    experts_all = exp_local * n_expert
    slots = min(MOST, tok_rows)

    experts = jnp.arange(experts_all, dtype=jnp.int32)
    hit = expert_ids.T[:, None, :] == experts[None, :, None]
    member = jnp.any(hit, axis=0)
    weight_of = jnp.sum(jnp.where(hit, combine_weights.T[:, None, :], 0.0), axis=0)
    order = jnp.arange(tok_rows, dtype=jnp.int32)
    earlier = (order[:, None] < order[None, :]).astype(jnp.bfloat16)
    rank = jnp.dot(member.astype(jnp.bfloat16), earlier, preferred_element_type=jnp.float32)
    place = jnp.where(member, rank.astype(jnp.int32), -1)
    lines = experts_all * tok_rows // tokens.shape[1]
    marks = place.astype(jnp.bfloat16).reshape(lines, tokens.shape[1])
    marks = jnp.pad(marks, ((0, MARK - lines), (0, 0)))
    marked = jnp.concatenate([tokens, marks], axis=0)
    across = tokens.shape[1] // (exp_local * tok_rows)
    me = lax.axis_index("expert")
    spot = jnp.stack([me // across, me % across]).astype(jnp.int32)

    seat = place[:, None, :] == jnp.arange(slots, dtype=jnp.int32)[None, :, None]
    spread = jnp.where(seat, weight_of[:, None, :], 0.0).reshape(experts_all * slots, tok_rows)
    high = spread.astype(jnp.bfloat16)
    low = (spread - high.astype(jnp.float32)).astype(jnp.bfloat16)

    cols = down_weight.shape[2] // n_width
    cut = jnp.stack([down_weight[:, :, n * cols : (n + 1) * cols] for n in range(n_width)])
    weights = lax.all_to_all(cut, "width", split_axis=0, concat_axis=0, tiled=True)

    ids = chunk_ids()
    send = lambda v, by: lax.ppermute(v, "expert", move(1, by))
    swap = lambda v: lax.ppermute(v, "expert", other_core())
    crossed = lambda a, b: [a, swap(a), b, swap(b)]
    compute = lambda parts: gate_up(spot, parts, gate_weight, up_weight, slots, tok_rows)
    near, (fore_a, back_a), (fore_b, back_b) = near_chunks(marked)
    first = compute(crossed(*near))
    parts, first = lax.optimization_barrier((crossed(fore_a, back_a), first))
    second = compute(parts)
    fore_b, back_b, weights, second = lax.optimization_barrier((fore_b, back_b, weights, second))
    far_a, far_b = send(fore_a, 1), send(back_b, -1)
    third = compute(crossed(fore_b, back_b))
    far_a, far_b, third = lax.optimization_barrier((far_a, far_b, third))
    fourth = compute(crossed(far_a, far_b))
    ring = lambda h: [h, around(h, 1), around(h, -1), around(h, 2)]
    last = ring(fourth)
    hidden = [lax.all_gather(h, "width", axis=0, tiled=False) for h in (first, second)]
    hidden.append(ring(third))
    mine = lax.axis_index("width").astype(jnp.int32)[None]
    at = lambda v: jnp.concatenate([v.reshape(-1), mine])
    rows = down(at(jnp.concatenate([ids[0], ids[2]])), [hidden[0], hidden[2]], weights, n_expert)
    rows = down(at(jnp.concatenate([ids[1], ids[3]])), [hidden[1], last], weights, n_expert, rows)

    returned = lax.all_to_all(rows, "expert", split_axis=0, concat_axis=0, tiled=True)
    returned = returned.reshape(experts_all * slots, cols)
    both = jnp.concatenate([high, low], axis=1)
    mixed = lax.dot_general(
        both, returned, (((0,), (0,)), ((), ())), preferred_element_type=jnp.float32
    )
    return (mixed[:tok_rows] + mixed[tok_rows:]).astype(jnp.bfloat16)


def solution(mesh):
    placed = (
        P("expert", None),
        P("expert", None),
        P("expert", None),
        P("expert", None, "width"),
        P("expert", None, "width"),
        P("expert", "width", None),
    )
    return jax.shard_map(
        local, mesh=mesh, in_specs=placed, out_specs=P("expert", "width"), check_vma=False
    )
```

```python
import jax
import jax.numpy as jnp
from jax import lax
from jax.experimental import pallas as pl
from jax.experimental.pallas import tpu as pltpu
from jax.sharding import PartitionSpec as P

MOST = 32
SIDE = 4
STEPS = 2
RING = (0, 3, 1, 2)
MARK = 8
VMEM_BYTES = 56 * 1024 * 1024


def gate_up_body(slots, tok, each, at_ref, *refs):
    parts, marks = refs[:4], refs[4 : 4 + 4 * each]
    gate_ref, up_ref, out_ref, rows_ref, acc_ref = refs[4 + 4 * each :]
    step = pl.program_id(0)
    exp_local = gate_ref.shape[0]
    block = parts[0].shape[0] // each
    place = lax.broadcasted_iota(jnp.int32, (slots, tok), 0)

    @pl.when(step == 0)
    def _():
        acc_ref[...] = jnp.zeros_like(acc_ref)

    for b in range(4 * each):
        mark = marks[b][...].astype(jnp.int32)
        seats = mark[0:1]
        for r in range(1, mark.shape[0]):
            seats = jnp.where(at_ref[0] == r, mark[r : r + 1], seats)
        pick = jnp.concatenate(
            [
                jnp.where(place == seats[:, j * tok : (j + 1) * tok], 1.0, 0.0).astype(
                    jnp.bfloat16
                )
                for j in range(exp_local)
            ],
            axis=0,
        )
        at = (b % each) * block
        rows = jnp.dot(
            pick, parts[b // each][at : at + tok, :], preferred_element_type=jnp.float32
        ).astype(jnp.bfloat16)
        for j in range(exp_local):
            rows_ref[j, b * slots : (b + 1) * slots, :] = rows[j * slots : (j + 1) * slots]
    for j in range(exp_local):
        joined = jnp.concatenate([gate_ref[j], up_ref[j]], axis=1)
        acc_ref[j] += jnp.dot(rows_ref[j], joined, preferred_element_type=jnp.float32)

    @pl.when(step == pl.num_programs(0) - 1)
    def _():
        for j in range(exp_local):
            hid = gate_ref.shape[-1]
            hidden = (jax.nn.silu(acc_ref[j, :, :hid]) * acc_ref[j, :, hid:]).astype(jnp.bfloat16)
            out_ref[:, j] = hidden.reshape(4 * each, slots, hid)


def gate_up(spot, parts, gate_weight, up_weight, slots, tok):
    exp_local, width_all, hid = gate_weight.shape
    block = tok + MARK
    each = parts[0].shape[0] // block
    count = 4 * each
    wide = width_all // STEPS
    weight_spec = pl.BlockSpec((exp_local, wide, hid), lambda k, at: (0, k, 0))
    part_spec = pl.BlockSpec((parts[0].shape[0], wide), lambda k, at: (0, k))
    mark_specs = [
        pl.BlockSpec(
            (MARK, exp_local * tok),
            lambda k, at, b=b: (b * (block // MARK) + tok // MARK, at[1]),
        )
        for b in range(each)
    ]
    marks = [part for part in parts for _ in range(each)]
    return pl.pallas_call(
        lambda *refs: gate_up_body(slots, tok, each, *refs),
        out_shape=jax.ShapeDtypeStruct((count, exp_local, slots, hid), jnp.bfloat16),
        grid_spec=pltpu.PrefetchScalarGridSpec(
            num_scalar_prefetch=1,
            grid=(STEPS,),
            in_specs=[*[part_spec] * 4, *mark_specs * 4, weight_spec, weight_spec],
        out_specs=pl.BlockSpec((count, exp_local, slots, hid), lambda k, at: (0, 0, 0, 0)),
            scratch_shapes=[
                pltpu.VMEM((exp_local, count * slots, wide), jnp.bfloat16),
                pltpu.VMEM((exp_local, count * slots, 2 * hid), jnp.float32),
            ],
        ),
        compiler_params=pltpu.CompilerParams(vmem_limit_bytes=VMEM_BYTES),
        cost_estimate=pl.CostEstimate(flops=1, transcendentals=0, bytes_accessed=1),
        name="gate_up",
    )(spot, *parts, *marks, gate_weight, up_weight)


def down_body(counts, ids_ref, *refs):
    refs = list(refs)
    out_ref, rows_ref, sem = refs[-3:]
    mine = ids_ref[rows_ref.shape[0]]
    sets = []
    for count in counts:
        sets.append([refs.pop(0)] if count else [refs.pop(0) for _ in RING])
    w_ref = refs[0]
    n_width, exp_local, hid, cols = w_ref.shape
    copies, base = [], 0
    for count, hs in zip(counts, sets):
        blocks, _, slots, _ = hs[0].shape[-4:]
        for j in range(exp_local):
            if count:
                rows = [hs[0][y, :, j].reshape(blocks * slots, hid) for y in range(n_width)]
                weight = [w_ref[y, j] for y in range(n_width)]
            else:
                rows = [h[:, j].reshape(blocks * slots, hid) for h in hs]
                weight = [w_ref[lax.rem(mine + by, n_width), j] for by in RING]
            total = jnp.dot(
                jnp.concatenate(rows, axis=1),
                jnp.concatenate(weight, axis=0),
                preferred_element_type=jnp.float32,
            )
            rows_ref[base : base + blocks, j] = total.astype(jnp.bfloat16).reshape(
                blocks, slots, cols
            )
        for b in range(base, base + blocks):
            copy = pltpu.make_async_copy(rows_ref.at[b], out_ref.at[ids_ref[b]], sem.at[b])
            copy.start()
            copies.append(copy)
        base += blocks
    for copy in copies:
        copy.wait()


def down(ids, hidden, weights, sources, before=None):
    counts = [0 if isinstance(h, list) else h.shape[1] for h in hidden]
    flat = [v for h in hidden for v in (h if isinstance(h, list) else [h])]
    exp_local, slots = flat[0].shape[-3:-1]
    blocks = sum(h[0].shape[0] if isinstance(h, list) else h.shape[1] for h in hidden)
    cols = weights.shape[-1]
    operands = [ids, *flat, weights]
    specs = [pl.BlockSpec(memory_space=pltpu.VMEM)] * (len(flat) + 1)
    aliases = {}
    if before is not None:
        aliases = {len(operands): 0}
        operands.append(before)
        specs = specs + [pl.BlockSpec(memory_space=pl.ANY)]
    return pl.pallas_call(
        lambda *refs: down_body(counts, *refs),
        out_shape=jax.ShapeDtypeStruct((sources, exp_local, slots, cols), jnp.bfloat16),
        grid_spec=pltpu.PrefetchScalarGridSpec(
            num_scalar_prefetch=1,
            grid=(),
            in_specs=specs,
            out_specs=pl.BlockSpec(memory_space=pl.ANY),
            scratch_shapes=[
                pltpu.VMEM((blocks, exp_local, slots, cols), jnp.bfloat16),
                pltpu.SemaphoreType.DMA((blocks,)),
            ],
        ),
        input_output_aliases=aliases,
        compiler_params=pltpu.CompilerParams(vmem_limit_bytes=VMEM_BYTES),
        cost_estimate=pl.CostEstimate(flops=1, transcendentals=0, bytes_accessed=1),
        name="down",
    )(*operands)


def place_of(z, x, c):
    return (z % SIDE) * SIDE * 2 + (x % SIDE) * 2 + c


def move(axis, by):
    pairs = []
    for z in range(SIDE):
        for x in range(SIDE):
            for c in range(2):
                along_z = (axis == 0) == (c == 0)
                to = place_of(z + by, x, c) if along_z else place_of(z, x + by, c)
                pairs.append((place_of(z, x, c), to))
    return pairs


def other_core():
    spots = [(z, x, c) for z in range(SIDE) for x in range(SIDE) for c in range(2)]
    return [(place_of(z, x, c), place_of(z, x, 1 - c)) for z, x, c in spots]


def near_chunks(tokens):
    half = tokens.shape[0] // (2 * MARK) * MARK
    send = lambda v, axis, by: lax.ppermute(v, "expert", move(axis, by))
    fore, back = send(tokens, 0, 1), send(tokens, 0, -1)
    fore, back = lax.optimization_barrier((fore, back))
    far = [send(fore[:half], 0, 1), send(back[half:], 0, -1)]
    near_a = jnp.concatenate([tokens, fore], axis=0)
    near_b = jnp.concatenate([back, *far], axis=0)
    fore_a, back_a = send(near_a, 1, 1), send(near_a, 1, -1)
    fore_b, back_b = send(near_b, 1, 1), send(near_b, 1, -1)
    return (near_a, near_b), (fore_a, back_a), (fore_b, back_b)


def chunk_ids():
    me = lax.axis_index("expert")
    z, x, c = me // (2 * SIDE), me // 2 % SIDE, me % 2
    near, wide = (0, -1), (1, 2)
    chunks = [
        ((near, 0), (wide, 0)),
        ((near, -1), (near, 1)),
        ((wide, -1), (wide, 1)),
        ((near, -2), (wide, 2)),
    ]
    first, second, kinds = [], [], []
    for halves in chunks:
        for along, across in halves:
            for kind in (0, 1):
                for step in along:
                    first.append(step)
                    second.append(across)
                    kinds.append(kind)
    first, second, kinds = (jnp.array(v, jnp.int32) for v in (first, second, kinds))
    core = jnp.where(kinds == 0, c, 1 - c)
    dz = jnp.where(core == 0, first, second)
    dx = jnp.where(core == 0, second, first)
    ids = (z + dz + SIDE) % SIDE * (2 * SIDE) + (x + dx + SIDE) % SIDE * 2 + core
    return ids.astype(jnp.int32).reshape(4, -1)


def around(v, by):
    n = lax.axis_size("width")
    return lax.ppermute(v, "width", [(i, (i + by) % n) for i in range(n)])


def local(tokens, expert_ids, combine_weights, gate_weight, up_weight, down_weight):
    tok_rows = tokens.shape[0]
    exp_local = gate_weight.shape[0]
    n_expert = lax.axis_size("expert")
    n_width = lax.axis_size("width")
    experts_all = exp_local * n_expert
    slots = min(MOST, tok_rows)

    experts = jnp.arange(experts_all, dtype=jnp.int32)
    hit = expert_ids.T[:, None, :] == experts[None, :, None]
    member = jnp.any(hit, axis=0)
    weight_of = jnp.sum(jnp.where(hit, combine_weights.T[:, None, :], 0.0), axis=0)
    order = jnp.arange(tok_rows, dtype=jnp.int32)
    earlier = (order[:, None] < order[None, :]).astype(jnp.bfloat16)
    rank = jnp.dot(member.astype(jnp.bfloat16), earlier, preferred_element_type=jnp.float32)
    place = jnp.where(member, rank.astype(jnp.int32), -1)
    lines = experts_all * tok_rows // tokens.shape[1]
    marks = place.astype(jnp.bfloat16).reshape(lines, tokens.shape[1])
    marks = jnp.pad(marks, ((0, MARK - lines), (0, 0)))
    marked = jnp.concatenate([tokens, marks], axis=0)
    across = tokens.shape[1] // (exp_local * tok_rows)
    me = lax.axis_index("expert")
    spot = jnp.stack([me // across, me % across]).astype(jnp.int32)

    seat = place[:, None, :] == jnp.arange(slots, dtype=jnp.int32)[None, :, None]
    spread = jnp.where(seat, weight_of[:, None, :], 0.0).reshape(experts_all * slots, tok_rows)
    high = spread.astype(jnp.bfloat16)
    low = (spread - high.astype(jnp.float32)).astype(jnp.bfloat16)

    cols = down_weight.shape[2] // n_width
    cut = jnp.stack([down_weight[:, :, n * cols : (n + 1) * cols] for n in range(n_width)])
    weights = lax.all_to_all(cut, "width", split_axis=0, concat_axis=0, tiled=True)

    ids = chunk_ids()
    send = lambda v, by: lax.ppermute(v, "expert", move(1, by))
    swap = lambda v: lax.ppermute(v, "expert", other_core())
    crossed = lambda a, b: [a, swap(a), b, swap(b)]
    compute = lambda parts: gate_up(spot, parts, gate_weight, up_weight, slots, tok_rows)
    near, (fore_a, back_a), (fore_b, back_b) = near_chunks(marked)
    first = compute(crossed(*near))
    parts, first = lax.optimization_barrier((crossed(fore_a, back_a), first))
    second = compute(parts)
    fore_b, back_b, weights, second = lax.optimization_barrier((fore_b, back_b, weights, second))
    far_a, far_b = send(fore_a, 1), send(back_b, -1)
    third = compute(crossed(fore_b, back_b))
    far_a, far_b, third = lax.optimization_barrier((far_a, far_b, third))
    fourth = compute(crossed(far_a, far_b))
    ring = lambda h: [h, around(h, 1), around(h, -1), around(h, 2)]
    last = ring(fourth)
    hidden = [lax.all_gather(h, "width", axis=0, tiled=False) for h in (first, second)]
    hidden.append(ring(third))
    mine = lax.axis_index("width").astype(jnp.int32)[None]
    at = lambda v: jnp.concatenate([v.reshape(-1), mine])
    rows = down(at(jnp.concatenate([ids[0], ids[2]])), [hidden[0], hidden[2]], weights, n_expert)
    rows = down(at(jnp.concatenate([ids[1], ids[3]])), [hidden[1], last], weights, n_expert, rows)

    returned = lax.all_to_all(rows, "expert", split_axis=0, concat_axis=0, tiled=True)
    returned = returned.reshape(experts_all * slots, cols)
    both = jnp.concatenate([high, low], axis=1)
    mixed = lax.dot_general(
        both, returned, (((0,), (0,)), ((), ())), preferred_element_type=jnp.float32
    )
    return (mixed[:tok_rows] + mixed[tok_rows:]).astype(jnp.bfloat16)


def solution(mesh):
    placed = (
        P("expert", None),
        P("expert", None),
        P("expert", None),
        P("expert", None, "width"),
        P("expert", None, "width"),
        P("expert", "width", None),
    )
    return jax.shard_map(
        local, mesh=mesh, in_specs=placed, out_specs=P("expert", "width"), check_vma=False
    )
```
